32 devices in a mesh: fsdp: 4 (over z), etp: 2 (over y), rep: 4 (over x, core).
Axes of the slice: x: 2, y: 2, z: 4, core: 2. Of those that a mesh axis runs over, the one named last changes fastest.
Arguments:
- hidden_rows: bfloat16 [4096, 2048], P(('fsdp', 'rep'), 'etp'), may hold values from -6 to 6
- pair_expert: int32 [4096], P(('fsdp', 'rep')), may hold values from 1 to 7
- live_blocks: int32 [16], P(('fsdp', 'rep')), may hold values from 1 to 2, as said below
- router_weight: bfloat16 [2048, 8], replicated, may hold values from -0.125 to 0.125
- gate_weight: bfloat16 [2048, 7168], P('fsdp', 'etp'), may hold values from -0.125 to 0.125
- up_weight: bfloat16 [2048, 7168], P('fsdp', 'etp'), may hold values from -0.125 to 0.125
- down_weight: bfloat16 [2048, 7168], P('fsdp', 'etp'), may hold values from -0.0625 to 0.0625
- output_grad: bfloat16 [4096, 2048], P(('fsdp', 'rep'), 'etp'), may hold values from -0.59765625 to 0.59765625
Outputs:
- expert_out: bfloat16 [4096, 2048], P(('fsdp', 'rep'), 'etp')
- rows_grad: bfloat16 [4096, 2048], P(('fsdp', 'rep'), 'etp')
- gate_grad: bfloat16 [2048, 7168], P('fsdp', 'etp')
- up_grad: bfloat16 [2048, 7168], P('fsdp', 'etp')
- down_grad: bfloat16 [2048, 7168], P('fsdp', 'etp')
- router_grad: float32 [2048, 8], P('etp')
The draws below stay inside these ranges and needn't reach their ends.
Inputs may be any that keep to these rules, and one draw needn't show every extreme that they name: live_blocks[g] counts the live 128-row blocks at the head of group g's 256 row slots; the slots after them are padding; some group has all 2 blocks live. `pair_expert`: each row's second expert; expert 0 is the expert computed here.
All inputs are finite; a program needn't handle non-finite values.
Results may differ from the reference program's by a relative error of at most 0.015.
Values may be sent and summed in bfloat16 or wider, within the bound.
No kernel may reach another device: no remote copies, remote signals or barrier semaphores. Data moves between devices by JAX's collectives and lax.ppermute only.
A program may use at most 256 MiB of HBM per device.

```python
import jax
import jax.numpy as jnp
from jax import lax

DM = 2048
FFW = 7168
EXPERTS = 8
BLOCK = 128
BLOCKS = 2
ROWS_DEV = 256
GROUPS = 16
ROWS = 4096


def draw_live_blocks(key, part):
    first_key, second_key, third_key = jax.random.split(jax.random.fold_in(key, 17), 3)
    extra = jax.random.randint(first_key, (GROUPS,), 0, BLOCKS)
    chosen = jax.random.randint(second_key, (GROUPS,), 0, 3) == 0
    counts = 1 + jnp.where(chosen, extra, 0)
    fullest = jax.random.randint(third_key, (), 0, GROUPS)
    counts = counts.at[fullest].set(BLOCKS)
    return counts.astype(jnp.int32)


def touch_ends(values, stream_key, low, top_value):
    spot = [jax.random.randint(jax.random.fold_in(stream_key, axis), (), 0, length) for axis, length in enumerate(values.shape)]
    main_axis = values.shape.index(max(values.shape))
    beside = spot[:main_axis] + [(spot[main_axis] + 1) % values.shape[main_axis]] + spot[main_axis + 1:]
    return values.at[tuple(spot)].set(low).at[tuple(beside)].set(top_value)


def level_of(own_key, shape, shards, smallest, high):
    loudness = 1.0
    for position, blocks in shards:
        heights = jax.random.uniform(jax.random.fold_in(jax.random.fold_in(own_key, 6), position), (blocks,), jnp.float32, smallest / len(shards), high / len(shards))
        loudness = loudness * jnp.repeat(jnp.exp(heights), shape[position] // blocks).reshape((-1,) + (1,) * (len(shape) - 1 - position))
    return loudness


def noise(stream_key, shape, spread, most, cuts=(), kind=jnp.bfloat16):
    level = level_of(stream_key, shape, cuts, -0.22, 0.18) if cuts else 1.0
    array = jax.random.normal(stream_key, shape, jnp.float32) * spread * level
    return jnp.minimum(jnp.maximum(array, -most), most).astype(kind)


def setup_inputs(seed: int = 0) -> dict:
    seeds = jax.random.split(jax.random.key(seed), 9)
    hidden_rows = noise(seeds[0], (ROWS, DM), 1.0, 6.0, ((0, 16), (1, 2)))
    pair_expert = touch_ends(jax.random.randint(seeds[1], (ROWS,), 1, EXPERTS), jax.random.fold_in(seeds[1], 1), 1, EXPERTS - 1).astype(jnp.int32)
    live_blocks = draw_live_blocks(jax.random.fold_in(seeds[8], 71), 0)
    router_weight = noise(seeds[3], (DM, EXPERTS), DM ** -0.5, 0.125)
    gate_weight = noise(seeds[4], (DM, FFW), DM ** -0.5, 0.125, ((0, 4), (1, 2)))
    up_weight = noise(seeds[5], (DM, FFW), DM ** -0.5, 0.125, ((0, 4), (1, 2)))
    down_weight = noise(seeds[6], (DM, FFW), FFW ** -0.5, 0.0625, ((0, 4), (1, 2)))
    output_grad = noise(seeds[7], (ROWS, DM), 0.1, 0.59765625, ((0, 16), (1, 2)))
    return dict(hidden_rows=hidden_rows, pair_expert=pair_expert, live_blocks=live_blocks, router_weight=router_weight, gate_weight=gate_weight, up_weight=up_weight, down_weight=down_weight, output_grad=output_grad)


OUTER_DIMS = (((0,), (0,)), ((), ()))
INNER_DIMS = (((1,), (1,)), ((), ()))


def reference(hidden_rows, pair_expert, live_blocks, router_weight, gate_weight, up_weight, down_weight, output_grad):
    slot_index = jnp.arange(ROWS, dtype=jnp.int32) % ROWS_DEV
    live_rows = jnp.repeat(live_blocks, ROWS_DEV) * BLOCK
    alive_mask = (slot_index < live_rows).astype(jnp.float32)
    logits = jnp.dot(hidden_rows, router_weight, preferred_element_type=jnp.float32)
    picked = (pair_expert[:, None] == jnp.arange(EXPERTS, dtype=jnp.int32)[None, :]).astype(jnp.float32)
    margin = logits[:, 0] - jnp.sum(logits * picked, axis=1)
    weight_share = jax.nn.sigmoid(margin) * alive_mask
    gate_pre = jnp.dot(hidden_rows, gate_weight, preferred_element_type=jnp.float32)
    up_pre = jnp.dot(hidden_rows, up_weight, preferred_element_type=jnp.float32)
    activated = jax.nn.silu(gate_pre)
    hidden = (activated * up_pre).astype(jnp.bfloat16)
    full_out = lax.dot_general(hidden, down_weight, INNER_DIMS, preferred_element_type=jnp.float32)
    expert_out = (weight_share[:, None] * full_out).astype(jnp.bfloat16)
    mixing = jnp.sum(output_grad.astype(jnp.float32) * full_out, axis=1)
    margin_grad = mixing * weight_share * (1.0 - weight_share)
    scaled = (weight_share[:, None] * output_grad.astype(jnp.float32)).astype(jnp.bfloat16)
    hidden_grad = jnp.dot(scaled, down_weight, preferred_element_type=jnp.float32)
    sigmoid_gate = jax.nn.sigmoid(gate_pre)
    gate_delta = (hidden_grad * up_pre * sigmoid_gate * (1.0 + gate_pre * (1.0 - sigmoid_gate))).astype(jnp.bfloat16)
    up_delta = (hidden_grad * activated).astype(jnp.bfloat16)
    back_sum = lax.dot_general(gate_delta, gate_weight, INNER_DIMS, preferred_element_type=jnp.float32)
    back_sum = back_sum + lax.dot_general(up_delta, up_weight, INNER_DIMS, preferred_element_type=jnp.float32)
    router_float = router_weight.astype(jnp.float32)
    router_gap = router_float[:, 0][None, :] - jnp.dot(picked, router_float.T, precision=lax.Precision.HIGHEST)
    rows_grad = (back_sum + margin_grad[:, None] * router_gap).astype(jnp.bfloat16)
    first_expert = (jnp.arange(EXPERTS, dtype=jnp.int32) == 0).astype(jnp.float32)
    margin_coef = margin_grad[:, None] * (first_expert[None, :] - picked)
    router_grad = jnp.dot(hidden_rows.astype(jnp.float32).T, margin_coef, precision=lax.Precision.HIGHEST)

    def group_terms(totals, group):
        row_start = (group * ROWS_DEV).astype(jnp.int32)
        inputs_g = lax.dynamic_slice_in_dim(hidden_rows, row_start, ROWS_DEV, 0)
        gate_g = lax.dynamic_slice_in_dim(gate_delta, row_start, ROWS_DEV, 0)
        up_g = lax.dynamic_slice_in_dim(up_delta, row_start, ROWS_DEV, 0)
        scaled_g = lax.dynamic_slice_in_dim(scaled, row_start, ROWS_DEV, 0)
        hidden_g = lax.dynamic_slice_in_dim(hidden, row_start, ROWS_DEV, 0)
        terms = (
            lax.dot_general(inputs_g, gate_g, OUTER_DIMS, preferred_element_type=jnp.float32),
            lax.dot_general(inputs_g, up_g, OUTER_DIMS, preferred_element_type=jnp.float32),
            lax.dot_general(scaled_g, hidden_g, OUTER_DIMS, preferred_element_type=jnp.float32),
        )
        rounded = tuple(lax.optimization_barrier(term.astype(jnp.bfloat16)).astype(jnp.float32) for term in terms)
        return tuple(total + piece_sum for total, piece_sum in zip(totals, rounded)), None

    zeros = jnp.zeros((DM, FFW), jnp.float32)
    totals, unused = lax.scan(group_terms, (zeros, zeros, zeros), jnp.arange(GROUPS, dtype=jnp.int32))
    return (expert_out, rows_grad, totals[0].astype(jnp.bfloat16), totals[1].astype(jnp.bfloat16),
            totals[2].astype(jnp.bfloat16), router_grad)
```

```python
import jax
import jax.numpy as jnp
from jax import lax
from jax.experimental import pallas as pl
from jax.experimental.pallas import tpu as pltpu
from jax.sharding import PartitionSpec as P

BLOCK = 128
F32 = jnp.float32
BF16 = jnp.bfloat16


INNER = (((1,), (1,)), ((), ()))
OUTER = (((0,), (0,)), ((), ()))


def dot_nn(a, b):
    return jnp.dot(a, b, preferred_element_type=F32)


def dot_nt(a, b):
    return lax.dot_general(a, b, INNER, preferred_element_type=F32)


def dot_tn(a, b):
    return lax.dot_general(a, b, OUTER, preferred_element_type=F32)


def after(values, *others):
    return lax.optimization_barrier((values, others))[0]


def from_ahead(value, axis, size, step):
    return lax.ppermute(value, axis, [((i + step) % size, i) for i in range(size)])


def swap_bit(value, axis, size, bit):
    return lax.ppermute(value, axis, [(i, i ^ bit) for i in range(size)])


def place(sources, height, width, down, across):
    count = len(sources)
    if height % 16 or width % 128:
        out = jnp.zeros((down * height, across * width), sources[0][0].dtype)
        for array, index, row, column in sources:
            if array.ndim == 3:
                array = array[index[0]]
            elif index is not None:
                array = lax.dynamic_slice(
                    array, (index[0] * height, index[1] * width), (height, width)
                )
            out = lax.dynamic_update_slice(out, array, (row * height, column * width))
        return out

    table = []
    specs = []
    for array, index, row, column in sources:
        table += [row, column]
    for s, (array, index, row, column) in enumerate(sources):
        if array.ndim == 3:
            lead = index[0]
            specs.append(
                pl.BlockSpec((1, height, width), lambda i, p, lead=lead: (lead, 0, 0))
            )
        elif index is None:
            specs.append(pl.BlockSpec((height, width), lambda i, p: (0, 0)))
        else:
            at = len(table)
            table += [index[0], index[1]]
            specs.append(pl.BlockSpec((height, width), lambda i, p, at=at: (p[at], p[at + 1])))

    def kernel(p_ref, *refs):
        out = refs[-1]
        step = pl.program_id(0)
        for s in range(count):

            @pl.when(step == s)
            def _(s=s):
                out[...] = refs[s][...].reshape(height, width)

    size = count * height * width * 2
    return pl.pallas_call(
        kernel,
        out_shape=jax.ShapeDtypeStruct((down * height, across * width), sources[0][0].dtype),
        grid_spec=pltpu.PrefetchScalarGridSpec(
            num_scalar_prefetch=1,
            grid=(count,),
            in_specs=specs,
            out_specs=pl.BlockSpec(
                (height, width), lambda i, p: (p[2 * i], p[2 * i + 1])
            ),
        ),
        cost_estimate=pl.CostEstimate(flops=0, bytes_accessed=2 * size, transcendentals=0),
        name="place",
    )(jnp.stack([jnp.asarray(v, jnp.int32) for v in table]), *[s[0] for s in sources])


def make_body(nz, ny, nr):
    assert nr == 4 and nz % ny == 0 and nz & (nz - 1) == 0
    per_slab = nz // ny
    high_bits = [1 << b for b in reversed(range(1, nz.bit_length() - 1))]

    def swap_x(value):
        return swap_bit(value, "rep", nr, 2)

    def swap_c(value):
        return swap_bit(value, "rep", nr, 1)

    def swap_z(value):
        return swap_bit(value, "fsdp", nz, 1)

    def butterfly_sum(value, axis, size):
        bit = 1
        while bit < size:
            value = value + swap_bit(value, axis, size, bit)
            bit *= 2
        return value

    def body(
        hidden_rows,
        pair_expert,
        live_blocks,
        router_weight,
        gate_weight,
        up_weight,
        down_weight,
        output_grad,
    ):
        rows, width = hidden_rows.shape
        feats, hid = gate_weight.shape
        experts = router_weight.shape[1]
        hb = hid // 4
        half = feats // 2
        zi = lax.axis_index("fsdp")
        yi = lax.axis_index("etp")
        ri = lax.axis_index("rep")
        xi, ci, z1 = ri // 2, ri % 2, zi % 2
        first = yi * per_slab

        alive = lax.iota(jnp.int32, rows) < live_blocks[0] * BLOCK
        code = jnp.where(alive, pair_expert, 0)
        codes = jnp.concatenate([code, swap_z(code)])
        codes = jnp.concatenate([codes, swap_x(codes)])

        def slabs_of(value):
            return [value] + [from_ahead(value, "etp", ny, k) for k in range(1, ny)]

        x_half = jnp.concatenate([hidden_rows, swap_z(hidden_rows)], axis=0)
        x_rows = jnp.concatenate([x_half, swap_x(x_half)], axis=0)
        x_all = jnp.concatenate(slabs_of(x_rows), axis=1)
        g_half = jnp.concatenate([output_grad, swap_z(output_grad)], axis=0)
        g_half = jnp.concatenate(slabs_of(g_half), axis=1)
        g_all = jnp.concatenate([g_half, swap_x(g_half)], axis=0)

        def fetch(weights):
            got = {}
            for k in range(1, nz):
                block = xi * 2 + (zi - k) % 2
                parts = [
                    lax.dynamic_slice(w, (ci * half, block * hb), (half, hb)) for w in weights
                ]
                here = from_ahead(jnp.stack(parts), "fsdp", nz, k)
                got[k] = (here, swap_c(here))
            return got

        def assemble(weight, got, index):
            block = xi * 2 + z1
            base = ((zi - first) % nz) * 2
            sources = [(weight, (h, block), base + h, 0) for h in range(2)]
            for k, (here, there) in got.items():
                base = ((zi + k - first) % nz) * 2
                sources.append((here, (index,), base + ci, 0))
                sources.append((there, (index,), base + 1 - ci, 0))
            return place(sources, half, hb, 2 * nz, 1)

        got_gate_up = fetch([gate_weight, up_weight])
        got_down = fetch([after(down_weight, [v[0] for v in got_gate_up.values()])])
        w_gate = assemble(gate_weight, got_gate_up, 0)
        w_up = assemble(up_weight, got_gate_up, 1)
        w_down = assemble(down_weight, got_down, 0)

        router_rel = jnp.concatenate(
            [
                lax.dynamic_slice_in_dim(router_weight, ((yi + k) % ny) * width, width, 0)
                for k in range(ny)
            ],
            axis=0,
        )
        logits = dot_nn(x_all, router_rel)
        picked = (codes[:, None] == lax.iota(jnp.int32, experts)[None, :]).astype(F32)
        margin = logits[:, 0] - jnp.sum(logits * picked, axis=1)
        share = jnp.where(codes > 0, jax.nn.sigmoid(margin), 0.0)

        gate_pre = dot_nn(x_all, w_gate)
        up_pre = dot_nn(x_all, w_up)
        sig = jax.nn.sigmoid(gate_pre)
        activated = gate_pre * sig
        hidden_f = activated * up_pre
        hidden = hidden_f.astype(BF16)
        hidden_w = (hidden_f * share[:, None]).astype(BF16)

        def part_of(grad, m, h):
            at = ((zi ^ m) - first) % nz
            return lax.dynamic_slice(
                grad.reshape(nz, 2, half, hb), (at, h, 0, 0), (1, 1, half, hb)
            ).reshape(1, half, hb)

        def reduce_start(grad):
            sent = jnp.concatenate([part_of(grad, m, 1 - ci) for m in range(nz)])
            kept = jnp.concatenate([part_of(grad, m, ci) for m in range(nz)])
            return kept, swap_c(sent)

        def reduce_high(kept, got):
            total = (kept.astype(F32) + got.astype(F32)).astype(BF16)
            for bit in high_bits:
                count = total.shape[0] // 2
                got = swap_bit(total[count:], "fsdp", nz, bit)
                total = (total[:count].astype(F32) + got.astype(F32)).astype(BF16)
            return total

        def spread_grad(total):
            mine, other = total[0], swap_z(total[1])
            pieces = {(0, 0, 0): mine, (0, 0, 1): other}
            for (c, x, z), value in list(pieces.items()):
                pieces[c, 1, z] = swap_x(value)
            for (c, x, z), value in list(pieces.items()):
                pieces[1, x, z] = swap_c(value)
            sources = [
                (value, None, ci ^ c, (xi ^ x) * 2 + (z1 ^ z))
                for (c, x, z), value in pieces.items()
            ]
            return place(sources, half, hb, 2, 4)

        def slab(weight, k):
            return weight[k * width : (k + 1) * width]

        def send_slabs(make):
            return [from_ahead(make(k).astype(BF16), "etp", ny, ny - k) for k in range(1, ny)]

        def reduce_rows(total, swap):
            count = total.shape[0] // 2
            return total[:count] + swap(total[count:].astype(BF16)).astype(F32)

        d_down = dot_tn(g_all, hidden_w).astype(BF16)
        red_down = reduce_start(d_down)

        def out_part(k):
            return dot_nt(hidden, slab(w_down, k))

        out_sent = send_slabs(out_part)
        hidden_grad = dot_nn(g_all, w_down) * share[:, None]
        gate_delta = (hidden_grad * up_pre * sig * (1.0 + gate_pre * (1.0 - sig))).astype(BF16)
        up_delta = (hidden_grad * activated).astype(BF16)
        d_gate = dot_tn(x_all, gate_delta).astype(BF16)
        red_gate = reduce_start(d_gate)
        d_up = dot_tn(x_all, up_delta).astype(BF16)
        red_up = reduce_start(d_up)

        def back_part(k):
            return dot_nt(gate_delta, slab(w_gate, k)) + dot_nt(up_delta, slab(w_up, k))

        back_sent = send_slabs(back_part)
        out_own = out_part(0)
        back_own = back_part(0)

        tot_down = reduce_high(*red_down)
        tot_gate = reduce_high(*red_gate)
        tot_up = reduce_high(*red_up)

        out_total = out_own
        for got in out_sent:
            out_total = out_total + got.astype(F32)
        local_out = reduce_rows(reduce_rows(out_total, swap_x), swap_z)
        back_total = back_own
        for got in back_sent:
            back_total = back_total + got.astype(F32)
        back_local = reduce_rows(reduce_rows(back_total, swap_x), swap_z)

        down_grad = spread_grad(tot_down)
        gate_grad = spread_grad(tot_gate)
        up_grad = spread_grad(tot_up)

        own_share = share[:rows]
        own_picked = (pair_expert[:, None] == lax.iota(jnp.int32, experts)[None, :]).astype(F32)
        mixing = butterfly_sum(
            jnp.sum(output_grad.astype(F32) * local_out, axis=1), "etp", ny
        )
        margin_grad = mixing * own_share * (1.0 - own_share)
        expert_out = (own_share[:, None] * local_out).astype(BF16)

        router_local = lax.dynamic_slice_in_dim(router_weight, yi * width, width, 0).astype(F32)
        router_gap = router_local[:, 0][None, :] - jnp.dot(
            own_picked, router_local.T, precision=lax.Precision.HIGHEST
        )
        rows_grad = (back_local + margin_grad[:, None] * router_gap).astype(BF16)
        first_expert = (lax.iota(jnp.int32, experts) == 0).astype(F32)
        margin_coef = margin_grad[:, None] * (first_expert[None, :] - own_picked)
        router_part = jnp.dot(
            hidden_rows.astype(F32).T, margin_coef, precision=lax.Precision.HIGHEST
        )
        router_grad = butterfly_sum(butterfly_sum(router_part, "rep", nr), "fsdp", nz)
        return (expert_out, rows_grad, gate_grad, up_grad, down_grad, router_grad)

    return body


def solution(mesh):
    sizes = mesh.shape
    body = make_body(sizes["fsdp"], sizes["etp"], sizes["rep"])
    row_spec = P(("fsdp", "rep"), "etp")
    lane_spec = P(("fsdp", "rep"))
    weight_spec = P("fsdp", "etp")
    in_specs = (
        row_spec,
        lane_spec,
        lane_spec,
        P(),
        weight_spec,
        weight_spec,
        weight_spec,
        row_spec,
    )
    out_specs = (row_spec, row_spec, weight_spec, weight_spec, weight_spec, P("etp", None))
    return jax.shard_map(body, mesh=mesh, in_specs=in_specs, out_specs=out_specs, check_vma=False)
```
